32 devices in a mesh: ctx: 16 (over z, y, x), head: 2 (over core).
Axes of the slice: x: 2, y: 2, z: 4, core: 2. Of those that a mesh axis runs over, the one named last changes fastest.
Arguments:
- queries: bfloat16 [8192, 1024], P('ctx', 'head'), may hold values from -6 to 6
- key_rows: bfloat16 [8192, 1024], P('ctx', 'head'), may hold values from -6 to 6
- value_rows: bfloat16 [8192, 1024], P('ctx', 'head'), may hold values from -6 to 6
- decay_rates: float32 [8], P('head'), as said below
- norm_gain: float32 [1024], P('head'), may hold values from 0.5 to 1.5
- out_grad: bfloat16 [8192, 1024], P('ctx', 'head'), may hold values from -6 to 6
Outputs:
- normed_out: bfloat16 [8192, 1024], P('ctx', 'head')
- query_grad: bfloat16 [8192, 1024], P('ctx', 'head')
- key_grad: bfloat16 [8192, 1024], P('ctx', 'head')
- value_grad: bfloat16 [8192, 1024], P('ctx', 'head')
The draws below stay inside these ranges and needn't reach their ends.
Inputs may be any that keep to these rules, and one draw needn't show every extreme that they name: `decay_rates`: each head's decay factor per token is exp(-rate).
All inputs are finite; a program needn't handle non-finite values.
Results may differ from the reference program's by a relative error of at most 0.005.
Values sent between devices are 32-bit elements; how exact they have to be, the bound alone decides.
A program may use at most 64 MiB of HBM per device.

```python
import jax
import jax.numpy as jnp
from jax import lax

DK = 128
BLOCK = 256
HEADS = 8
TOKENS = 8192


def draw_decay_rates(key, part):
    picker, slow_key, fast_key = jax.random.split(key, 3)
    share = 0.5
    slow_rates = jnp.exp(jax.random.uniform(slow_key, (HEADS,), jnp.float32, jnp.log(0.5 / TOKENS), jnp.log(2.0 / TOKENS)))
    fast_rates = jnp.exp(jax.random.uniform(fast_key, (HEADS,), jnp.float32, jnp.log(0.02), jnp.log(0.05)))
    chosen = jax.random.uniform(picker, (HEADS,), jnp.float32) < share
    return jnp.where(chosen, slow_rates, fast_rates)


def levels(key, dims, cuts, least, top_value):
    factor_of, own = 1.0, jax.random.fold_in(key, 6)
    for dim, shards_of in cuts:
        steps = jnp.exp(jax.random.uniform(jax.random.fold_in(own, dim), (shards_of,), jnp.float32, least / len(cuts), top_value / len(cuts)))
        factor_of = factor_of * jnp.repeat(steps, dims[dim] // shards_of).reshape([-1 if axis == dim else 1 for axis in range(len(dims))])
    return factor_of


def bell_draw(rng, dims, spread, most, pieces=(), kind=jnp.bfloat16):
    level = levels(rng, dims, pieces, -0.22, 0.18) if pieces else 1.0
    entries = jax.random.normal(rng, dims, jnp.float32) * spread * level
    return jnp.minimum(jnp.maximum(entries, -most), most).astype(kind)


def setup_inputs(seed: int = 0) -> dict:
    splits = jax.random.split(jax.random.key(seed), 7)
    return {
        "queries": bell_draw(splits[0], (TOKENS, HEADS * DK), 1.0, 6.0, ((0, 16), (1, 2))),
        "key_rows": bell_draw(splits[1], (TOKENS, HEADS * DK), 1.0, 6.0, ((0, 16), (1, 2))),
        "value_rows": bell_draw(splits[2], (TOKENS, HEADS * DK), 1.0, 6.0, ((0, 16), (1, 2))),
        "decay_rates": draw_decay_rates(jax.random.fold_in(splits[6], 71), 0),
        "norm_gain": jnp.clip(1.0 + 0.1 * jax.random.normal(splits[4], (HEADS * DK,), jnp.float32), 0.5, 1.5),
        "out_grad": bell_draw(splits[5], (TOKENS, HEADS * DK), 1.0, 6.0, ((0, 16), (1, 2))),
    }


highest = lax.Precision.HIGHEST
epsilon = 1e-06

def exact_product(form, left, right):
    return jnp.einsum(form, left.astype(jnp.float32), right.astype(jnp.float32), precision=highest)

def decay_tables(decay_rates, length):
    position = jnp.arange(length, dtype=jnp.float32)
    spacing = position[:, None] - position[None, :]
    weights = jnp.where(spacing[None] >= 0, jnp.exp(-decay_rates[:, None, None] * jnp.maximum(spacing, 0.0)[None]), 0.0)
    leading = jnp.exp(-decay_rates[None, :] * (position[:, None] + 1.0))
    trailing = jnp.exp(-decay_rates[None, :] * (length - 1.0 - position[:, None]))
    after_end = jnp.exp(-decay_rates[None, :] * (length - position[:, None]))
    from_start = jnp.exp(-decay_rates[None, :] * position[:, None])
    return (weights, leading, trailing, after_end, from_start)

def reference(queries, key_rows, value_rows, decay_rates, norm_gain, out_grad):
    token_count = queries.shape[0]
    head_count = decay_rates.shape[0]
    head_width = queries.shape[1] // head_count
    block_count = token_count // BLOCK
    weights, leading, trailing, after_end, from_start = decay_tables(decay_rates, BLOCK)
    full_decay = jnp.exp(-decay_rates * BLOCK)[:, None, None]

    def blocked(array):
        return array.reshape(block_count, BLOCK, head_count, head_width)
    query_blocks = blocked(queries)
    key_blocks = blocked(key_rows)
    value_blocks = blocked(value_rows)
    initial = jnp.zeros((head_count, head_width, head_width), jnp.float32)

    def advance(memory, blocks):
        query_rows, key_part, value_part = blocks
        scores = exact_product('ihd,jhd->hij', query_rows, key_part)
        attn_probs = (scores * weights).astype(jnp.bfloat16)
        inside = exact_product('hij,jhd->ihd', attn_probs, value_part)
        carried = exact_product('iha,hac->ihc', query_rows, memory) * leading[:, :, None]
        update = exact_product('jha,jhc->hac', key_part.astype(jnp.float32) * trailing[:, :, None], value_part)
        return (full_decay * memory + update, inside + carried)
    _, outputs = lax.scan(advance, initial, (query_blocks, key_blocks, value_blocks))
    flat = outputs.reshape(token_count, head_count * head_width)
    features = float(head_count * head_width)
    scale = lax.rsqrt(lax.optimization_barrier(jnp.sum(flat * flat, axis=1)) / features + epsilon)
    normed = flat * scale[:, None]
    normed_out = (normed * norm_gain[None, :]).astype(jnp.bfloat16)
    grad_normed = out_grad.astype(jnp.float32) * norm_gain[None, :]
    coeff = scale * lax.optimization_barrier(jnp.sum(grad_normed * flat, axis=1)) / features
    grad_attn = (scale[:, None] * (grad_normed - normed * coeff[:, None])).astype(jnp.bfloat16)
    grad_blocks = blocked(grad_attn)

    def forward_grad(memory, blocks):
        query_rows, key_part, value_part, grad_rows = blocks
        grad_scores = exact_product('ihc,jhc->hij', grad_rows, value_part)
        grad_probs = (grad_scores * weights).astype(jnp.bfloat16)
        query_part = exact_product('hij,jha->iha', grad_probs, key_part)
        query_part = query_part + exact_product('ihc,hac->iha', grad_rows, memory) * leading[:, :, None]
        update = exact_product('jha,jhc->hac', key_part.astype(jnp.float32) * trailing[:, :, None], value_part)
        return (full_decay * memory + update, query_part)
    _, query_grad = lax.scan(forward_grad, initial, (query_blocks, key_blocks, value_blocks, grad_blocks))

    def backward_grad(backlog, blocks):
        query_rows, key_part, value_part, grad_rows = blocks
        scores = exact_product('ihd,jhd->hij', query_rows, key_part)
        attn_probs = (scores * weights).astype(jnp.bfloat16)
        grad_scores = exact_product('ihc,jhc->hij', grad_rows, value_part)
        grad_probs = (grad_scores * weights).astype(jnp.bfloat16)
        key_out = exact_product('hij,iha->jha', grad_probs, query_rows)
        key_out = key_out + exact_product('jhc,hac->jha', value_part, backlog) * after_end[:, :, None]
        value_out = exact_product('hij,ihc->jhc', attn_probs, grad_rows)
        value_out = value_out + exact_product('jha,hac->jhc', key_part, backlog) * after_end[:, :, None]
        gathered = exact_product('iha,ihc->hac', query_rows.astype(jnp.float32) * from_start[:, :, None], grad_rows)
        return (full_decay * backlog + gathered, (key_out, value_out))
    _, (key_grad, value_grad) = lax.scan(backward_grad, initial, (query_blocks, key_blocks, value_blocks, grad_blocks), reverse=True)

    def flatten(array):
        return array.reshape(token_count, head_count * head_width).astype(jnp.bfloat16)
    return (normed_out, flatten(query_grad), flatten(key_grad), flatten(value_grad))
```

```python
import functools
import math

import jax
import jax.numpy as jnp
from jax import lax
from jax.experimental import pallas as pl
from jax.experimental.pallas import tpu as pltpu
from jax.sharding import PartitionSpec as P

BLOCK = 256
CHUNKS = 2
EPSILON = 1e-06
MESH = pl.DeviceIdType.MESH
F32 = jnp.float32
BF16 = jnp.bfloat16


def dot(a, b, ca, cb):
    return lax.dot_general(a, b, (((ca,), (cb,)), ((), ())), preferred_element_type=F32)


def split(a):
    high = a.astype(BF16)
    return high, (a - high.astype(F32)).astype(BF16)


def power(rate, count):
    return jnp.exp(jnp.full((1, 128), -rate * count, F32))


class Scan:
    def __init__(self, reverse, n, groups, hp, length, rates, parts, whole, got, tosend, fromprev,
                 back, landed, a_send, a_recv, b_send, b_recv, c_send, c_recv):
        self.reverse, self.n, self.hp, self.length = reverse, n, hp, length
        self.size, self.groups = n // groups, groups
        self.rates, self.parts, self.whole = rates, parts, whole
        self.got, self.tosend, self.fromprev, self.back, self.landed = got, tosend, fromprev, back, landed
        self.sems = (a_send, a_recv, b_send, b_recv, c_send, c_recv)
        me = lax.axis_index("ctx")
        self.z = me // self.size
        r = me - self.z * self.size
        self.base = self.z * self.size
        self.rank = self.size - 1 - r if reverse else r
        self.zl = groups - 1 - self.z if reverse else self.z
        self.next = me - self.size if reverse else me + self.size
        self.rows = [pl.ds(c * (128 // CHUNKS), 128 // CHUNKS) for c in range(CHUNKS)]

    def device(self, rank):
        return self.base + (self.size - 1 - rank if self.reverse else rank)

    def a_copy(self, off, c):
        t = lax.rem(self.rank + off, self.size)
        return pltpu.make_async_remote_copy(
            src_ref=self.parts.at[pl.ds(t * self.hp, self.hp), self.rows[c]],
            dst_ref=self.got.at[off - 1, :, self.rows[c]],
            send_sem=self.sems[0].at[off - 1, c], recv_sem=self.sems[1].at[off - 1, c],
            device_id={"ctx": self.device(t)}, device_id_type=MESH)

    def b_copy(self, c):
        return pltpu.make_async_remote_copy(
            src_ref=self.tosend.at[:, self.rows[c]], dst_ref=self.fromprev.at[:, self.rows[c]],
            send_sem=self.sems[2].at[c], recv_sem=self.sems[3].at[c],
            device_id={"ctx": self.next}, device_id_type=MESH)

    def c_copy(self, off, c):
        t = lax.rem(self.rank + off, self.size)
        return pltpu.make_async_remote_copy(
            src_ref=self.back.at[off - 1, :, self.rows[c]], dst_ref=self.landed.at[off - 1, :, self.rows[c]],
            send_sem=self.sems[4].at[off - 1, c], recv_sem=self.sems[5].at[off - 1, c],
            device_id={"ctx": self.device(t)}, device_id_type=MESH)

    def begin(self):
        for c in range(CHUNKS):
            for off in range(1, self.size):
                self.a_copy(off, c).start()

    def relay(self):
        size, hp = self.size, self.hp
        first = self.rank * hp
        source = [lax.rem(self.rank + size - off, size) for off in range(size)]
        target = [lax.rem(self.rank + off, size) for off in range(size)]
        coef = []
        for i in range(hp):
            step = self.rates[first + i] * float(self.length)
            total = [power(step, (size - 1 - e).astype(F32)) for e in source]
            pre = [[jnp.where(e < t, power(step, jnp.maximum(t - 1 - e, 0).astype(F32)), 0.0) for e in source]
                   for t in target]
            lead = [power(step, t.astype(F32)) for t in target]
            coef.append((total, pre, lead, power(step, float(size))))
        for c in range(CHUNKS):
            rows = self.rows[c]
            for off in range(1, size):
                self.a_copy(off, c).wait_recv()
            totals, prefixes = [], []
            for i in range(hp):
                total, pre, _, _ = coef[i]
                pieces = [self.parts[pl.ds(first + i, 1), rows][0]]
                pieces += [self.got[off - 1, i, rows] for off in range(1, size)]
                totals.append(sum(w * x for w, x in zip(total, pieces)))
                prefixes.append([sum(w * x for w, x in zip(pre[o], pieces)) for o in range(size)])

            @pl.when(self.zl == 0)
            def _():
                self.fromprev[:, rows] = jnp.zeros((hp, 128 // CHUNKS, 128), F32)

            @pl.when(self.zl > 0)
            def _():
                self.b_copy(c).wait_recv()

            for i in range(hp):
                self.tosend[i, rows] = coef[i][3] * self.fromprev[i, rows] + totals[i]

            @pl.when(self.zl < self.groups - 1)
            def _():
                self.b_copy(c).start()

            for off in list(range(1, size)) + [0]:
                for i in range(hp):
                    value = coef[i][2][off] * self.fromprev[i, rows] + prefixes[i][off]
                    if off:
                        self.back[off - 1, i, rows] = value
                    else:
                        self.whole[pl.ds(first + i, 1), rows] = value[None]
                if off:
                    self.c_copy(off, c).start()

    def finish(self):
        for c in range(CHUNKS):
            for off in range(1, self.size):
                self.c_copy(off, c).wait_recv()
                owner = lax.rem(self.rank + self.size - off, self.size)
                self.whole[pl.ds(owner * self.hp, self.hp), self.rows[c]] = self.landed[off - 1, :, self.rows[c]]

    def drain(self):
        for c in range(CHUNKS):
            for off in range(1, self.size):
                self.a_copy(off, c).wait_send()
                self.c_copy(off, c).wait_send()

            @pl.when(self.zl < self.groups - 1)
            def _():
                self.b_copy(c).wait_send()


def scan_scratch(size, hp, heads):
    state = lambda *lead: pltpu.VMEM(lead + (128, 128), F32)
    dma = pltpu.SemaphoreType.DMA
    return [
        state(heads), state(heads), state(size - 1, hp), state(hp), state(hp), state(size - 1, hp),
        state(size - 1, hp),
        dma((size - 1, CHUNKS)), dma((size - 1, CHUNKS)), dma((CHUNKS,)), dma((CHUNKS,)),
        dma((size - 1, CHUNKS)), dma((size - 1, CHUNKS)),
    ]


def kernel(n, m, groups, heads, rates, q_ref, k_ref, v_ref, gain_ref, og_ref,
           normed_ref, qg_ref, kg_ref, vg_ref,
           w_ref, p_ref, x_ref, do_ref, first_ref, last_ref, kacc_ref, vacc_ref,
           mine_ref, theirs_ref, h_send, h_recv, *scans):
    tokens = q_ref.shape[0]
    blocks = tokens // BLOCK
    size = n // groups
    hp = heads // size
    me, head = lax.axis_index("ctx"), lax.axis_index("head")
    half = len(scans) // 2
    make = functools.partial(Scan, n=n, groups=groups, hp=hp, length=tokens, rates=rates)
    names = ("parts", "whole", "got", "tosend", "fromprev", "back", "landed",
             "a_send", "a_recv", "b_send", "b_recv", "c_send", "c_recv")
    forward = make(reverse=False, **dict(zip(names, scans[:half])))
    backward = make(reverse=True, **dict(zip(names, scans[half:])))

    barrier = pltpu.get_barrier_semaphore()
    for off in range(1, size):
        pl.semaphore_signal(barrier, inc=1, device_id={"ctx": forward.device(lax.rem(forward.rank + off, size))},
                            device_id_type=MESH)
    for off in range(1, m):
        pl.semaphore_signal(barrier, inc=1, device_id={"head": lax.rem(head + off, m)}, device_id_type=MESH)

    @pl.when(forward.z > 0)
    def _():
        pl.semaphore_signal(barrier, inc=1, device_id={"ctx": me - size}, device_id_type=MESH)

    @pl.when(forward.z < groups - 1)
    def _():
        pl.semaphore_signal(barrier, inc=1, device_id={"ctx": me + size}, device_id_type=MESH)

    position = lax.broadcasted_iota(jnp.int32, (BLOCK, 128), 0).astype(F32)

    def at(ref, b, h):
        return ref[b * BLOCK:(b + 1) * BLOCK, h * 128:(h + 1) * 128]

    for h in range(heads):
        trailing = jnp.exp(-rates[h] * (BLOCK - 1.0 - position))
        full = power(rates[h], float(BLOCK))
        state = None
        for b in range(blocks):
            high, low = split(at(k_ref, b, h).astype(F32) * trailing)
            v = at(v_ref, b, h)
            update = dot(high, v, 0, 0) + dot(low, v, 0, 0)
            if b < blocks - 1:
                first_ref[b, h] = update
            state = update if state is None else full * state + update
        forward.parts[h] = state

    pl.semaphore_wait(barrier, size - 1 + m - 1 + jnp.minimum(forward.z, 1)
                      + jnp.minimum(groups - 1 - forward.z, 1))
    forward.begin()

    spacing = (lax.broadcasted_iota(jnp.int32, (BLOCK, BLOCK), 0)
               - lax.broadcasted_iota(jnp.int32, (BLOCK, BLOCK), 1))
    causal = spacing >= 0
    gap = jnp.maximum(spacing, 0).astype(F32)
    for h in range(heads):
        w = jnp.where(causal, jnp.exp(-rates[h] * gap), 0.0)
        w_ref[h] = w
        for b in range(blocks):
            p = (dot(at(q_ref, b, h), at(k_ref, b, h), 1, 1) * w).astype(BF16)
            p_ref[b, h] = p
            x_ref[b * BLOCK:(b + 1) * BLOCK, h * 128:(h + 1) * 128] = dot(p, at(v_ref, b, h), 1, 0)

    forward.relay()
    forward.finish()

    squares = [0.0] * blocks
    projection = [0.0] * blocks
    for h in range(heads):
        leading = jnp.exp(-rates[h] * (position + 1.0))
        full = power(rates[h], float(BLOCK))
        memory = forward.whole[h]
        gain = gain_ref[:, h * 128:(h + 1) * 128]
        for b in range(blocks):
            high, low = split(memory)
            q = at(q_ref, b, h)
            x = at(x_ref, b, h) + (dot(q, high, 1, 0) + dot(q, low, 1, 0)) * leading
            x_ref[b * BLOCK:(b + 1) * BLOCK, h * 128:(h + 1) * 128] = x
            squares[b] = squares[b] + x * x
            projection[b] = projection[b] + at(og_ref, b, h).astype(F32) * gain * x
            if b < blocks - 1:
                memory = full * memory + first_ref[b, h]

    lane = lax.broadcasted_iota(jnp.int32, (BLOCK, 128), 1)
    for b in range(blocks):
        pair = jnp.where(lane == 0, jnp.sum(squares[b], axis=1, keepdims=True),
                         jnp.sum(projection[b], axis=1, keepdims=True))
        mine_ref[:, b * BLOCK:(b + 1) * BLOCK] = pair.T[:8]

    def h_copy(off):
        return pltpu.make_async_remote_copy(
            src_ref=mine_ref, dst_ref=theirs_ref.at[off - 1], send_sem=h_send.at[off - 1],
            recv_sem=h_recv.at[off - 1], device_id={"head": lax.rem(head + off, m)}, device_id_type=MESH)

    for off in range(1, m):
        h_copy(off).start()
    for off in range(1, m):
        h_copy(off).wait_recv()
    sums = mine_ref[...]
    for off in range(1, m):
        sums = sums + theirs_ref[off - 1]
    features = float(heads * 128 * m)
    scale_row = lax.rsqrt(sums[0:1] / features + EPSILON)
    coeff_row = scale_row * sums[1:2] / features
    even = lax.broadcasted_iota(jnp.int32, (128, BLOCK), 0) == 0
    for b in range(blocks):
        cut = slice(b * BLOCK, (b + 1) * BLOCK)
        both = jnp.where(even, scale_row[:, cut], coeff_row[:, cut]).T
        scale = jnp.broadcast_to(both[:, 0:1], (BLOCK, 128))
        coeff = jnp.broadcast_to(both[:, 1:2], (BLOCK, 128))
        for h in range(heads):
            cols = slice(h * 128, (h + 1) * 128)
            gain = gain_ref[:, cols]
            normed = x_ref[cut, cols] * scale
            normed_ref[cut, cols] = (normed * gain).astype(BF16)
            g = at(og_ref, b, h).astype(F32) * gain
            do_ref[cut, cols] = (scale * (g - normed * coeff)).astype(BF16)

    for h in range(heads):
        start = jnp.exp(-rates[h] * position)
        full = power(rates[h], float(BLOCK))
        state = None
        for b in reversed(range(blocks)):
            high, low = split(at(q_ref, b, h).astype(F32) * start)
            do = at(do_ref, b, h)
            update = dot(high, do, 0, 0) + dot(low, do, 0, 0)
            if b > 0:
                last_ref[b - 1, h] = update
            state = update if state is None else full * state + update
        backward.parts[h] = state
    backward.begin()

    for h in range(heads):
        leading = jnp.exp(-rates[h] * (position + 1.0))
        full = power(rates[h], float(BLOCK))
        memory = forward.whole[h]
        w = w_ref[h]
        cols = slice(h * 128, (h + 1) * 128)
        for b in range(blocks):
            cut = slice(b * BLOCK, (b + 1) * BLOCK)
            high, low = split(memory)
            do, k, q = at(do_ref, b, h), at(k_ref, b, h), at(q_ref, b, h)
            s = (dot(do, at(v_ref, b, h), 1, 1) * w).astype(BF16)
            qg_ref[cut, cols] = (dot(s, k, 1, 0)
                                 + (dot(do, high, 1, 1) + dot(do, low, 1, 1)) * leading).astype(BF16)
            kacc_ref[cut, cols] = dot(s, q, 0, 0)
            vacc_ref[cut, cols] = dot(p_ref[b, h], do, 0, 0)
            if b < blocks - 1:
                memory = full * memory + first_ref[b, h]

    backward.relay()
    backward.finish()

    for h in range(heads):
        after = jnp.exp(-rates[h] * (BLOCK - position))
        full = power(rates[h], float(BLOCK))
        backlog = backward.whole[h]
        cols = slice(h * 128, (h + 1) * 128)
        for b in reversed(range(blocks)):
            cut = slice(b * BLOCK, (b + 1) * BLOCK)
            high, low = split(backlog)
            v, k = at(v_ref, b, h), at(k_ref, b, h)
            kg_ref[cut, cols] = (kacc_ref[cut, cols]
                                 + (dot(v, high, 1, 1) + dot(v, low, 1, 1)) * after).astype(BF16)
            vg_ref[cut, cols] = (vacc_ref[cut, cols]
                                 + (dot(k, high, 1, 0) + dot(k, low, 1, 0)) * after).astype(BF16)
            if b > 0:
                backlog = full * backlog + last_ref[b - 1, h]

    for off in range(1, m):
        h_copy(off).wait_send()
    forward.drain()
    backward.drain()


def solution(mesh):
    n, m = mesh.shape["ctx"], mesh.shape["head"]

    def on_device(queries, key_rows, value_rows, decay_rates, norm_gain, out_grad):
        tokens, width = queries.shape
        heads = decay_rates.shape[0]
        blocks = tokens // BLOCK
        size = math.gcd(heads, n)
        groups, hp = n // size, heads // size
        vmem = pl.BlockSpec(memory_space=pltpu.VMEM)
        out = jax.ShapeDtypeStruct((tokens, width), BF16)
        dma = pltpu.SemaphoreType.DMA
        return pl.pallas_call(
            functools.partial(kernel, n, m, groups, heads),
            out_shape=(out,) * 4,
            in_specs=[pl.BlockSpec(memory_space=pltpu.SMEM)] + [vmem] * 5,
            out_specs=(vmem,) * 4,
            scratch_shapes=[
                pltpu.VMEM((heads, BLOCK, BLOCK), F32),
                pltpu.VMEM((blocks, heads, BLOCK, BLOCK), BF16),
                pltpu.VMEM((tokens, width), F32),
                pltpu.VMEM((tokens, width), BF16),
                pltpu.VMEM((max(blocks - 1, 1), heads, 128, 128), F32),
                pltpu.VMEM((max(blocks - 1, 1), heads, 128, 128), F32),
                pltpu.VMEM((tokens, width), F32),
                pltpu.VMEM((tokens, width), F32),
                pltpu.VMEM((8, tokens), F32),
                pltpu.VMEM((max(m - 1, 1), 8, tokens), F32),
                dma((max(m - 1, 1),)), dma((max(m - 1, 1),)),
            ] + scan_scratch(size, hp, heads) * 2,
            compiler_params=pltpu.CompilerParams(
                collective_id=0, has_side_effects=True, vmem_limit_bytes=48 * 2**20),
        )(decay_rates, queries, key_rows, value_rows, norm_gain.reshape(1, width), out_grad)

    rows = P("ctx", "head")
    return jax.shard_map(
        on_device, mesh=mesh, in_specs=(rows, rows, rows, P("head"), P("head"), rows),
        out_specs=(rows,) * 4, check_vma=False)
```

```python
import functools
import math

import jax
import jax.numpy as jnp
from jax import lax
from jax.experimental import pallas as pl
from jax.experimental.pallas import tpu as pltpu
from jax.sharding import PartitionSpec as P

BLOCK = 256
CHUNKS = 2
EPSILON = 1e-06
MESH = pl.DeviceIdType.MESH
F32 = jnp.float32
BF16 = jnp.bfloat16


def dot(a, b, ca, cb):
    return lax.dot_general(a, b, (((ca,), (cb,)), ((), ())), preferred_element_type=F32)


def split(a):
    high = a.astype(BF16)
    return high, (a - high.astype(F32)).astype(BF16)


def power(rate, count):
    return jnp.exp(jnp.full((1, 128), -rate * count, F32))


class Scan:
    def __init__(self, reverse, n, groups, hp, length, rates, parts, whole, got, tosend, arrive, fromprev, local,
                 back, landed, a_send, a_recv, b_send, b_recv, c_send, c_recv):
        self.reverse, self.n, self.hp, self.length = reverse, n, hp, length
        self.size, self.groups = n // groups, groups
        self.rates, self.parts, self.whole = rates, parts, whole
        self.got, self.tosend, self.arrive, self.fromprev = got, tosend, arrive, fromprev
        self.local, self.back, self.landed = local, back, landed
        self.sems = (a_send, a_recv, b_send, b_recv, c_send, c_recv)
        me = lax.axis_index("ctx")
        self.z = me // self.size
        r = me - self.z * self.size
        self.base = self.z * self.size
        self.rank = self.size - 1 - r if reverse else r
        self.zl = groups - 1 - self.z if reverse else self.z
        self.me = me
        self.rows = [pl.ds(c * (128 // CHUNKS), 128 // CHUNKS) for c in range(CHUNKS)]

    def device(self, rank):
        return self.base + (self.size - 1 - rank if self.reverse else rank)

    def a_copy(self, off, c):
        t = lax.rem(self.rank + off, self.size)
        return pltpu.make_async_remote_copy(
            src_ref=self.parts.at[pl.ds(t * self.hp, self.hp), self.rows[c]],
            dst_ref=self.got.at[off - 1, :, self.rows[c]],
            send_sem=self.sems[0].at[off - 1, c], recv_sem=self.sems[1].at[off - 1, c],
            device_id={"ctx": self.device(t)}, device_id_type=MESH)

    def b_copy(self, dz, c):
        step = dz * self.size
        return pltpu.make_async_remote_copy(
            src_ref=self.tosend.at[:, self.rows[c]], dst_ref=self.arrive.at[dz - 1, :, self.rows[c]],
            send_sem=self.sems[2].at[dz - 1, c], recv_sem=self.sems[3].at[dz - 1, c],
            device_id={"ctx": self.me - step if self.reverse else self.me + step}, device_id_type=MESH)

    def c_copy(self, off, c):
        t = lax.rem(self.rank + off, self.size)
        return pltpu.make_async_remote_copy(
            src_ref=self.back.at[off - 1, :, self.rows[c]], dst_ref=self.landed.at[off - 1, :, self.rows[c]],
            send_sem=self.sems[4].at[off - 1, c], recv_sem=self.sems[5].at[off - 1, c],
            device_id={"ctx": self.device(t)}, device_id_type=MESH)

    def begin(self, h):
        if (h + 1) % self.hp:
            return
        owner = h // self.hp
        off = lax.rem(owner - self.rank + self.size, self.size)

        @pl.when(off > 0)
        def _():
            for c in range(CHUNKS):
                self.a_copy(off, c).start()

    def relay(self):
        size, hp = self.size, self.hp
        first = self.rank * hp
        source = [lax.rem(self.rank + size - off, size) for off in range(size)]
        target = [lax.rem(self.rank + off, size) for off in range(size)]
        coef = []
        for i in range(hp):
            step = self.rates[first + i] * float(self.length)
            total = [power(step, (size - 1 - e).astype(F32)) for e in source]
            pre = [[jnp.where(e < t, power(step, jnp.maximum(t - 1 - e, 0).astype(F32)), 0.0) for e in source]
                   for t in target]
            lead = [power(step, t.astype(F32)) for t in target]
            jump = [power(step, float(size * dz)) for dz in range(self.groups - 1)]
            coef.append((total, pre, lead, jump))
        self.fromprev[...] = jnp.zeros_like(self.fromprev)
        prefixes = []
        for c in range(CHUNKS):
            rows = self.rows[c]
            for off in range(1, size):
                self.a_copy(off, c).wait_recv()
            prefix = []
            for i in range(hp):
                total, pre, _, _ = coef[i]
                pieces = [self.parts[pl.ds(first + i, 1), rows][0]]
                pieces += [self.got[off - 1, i, rows] for off in range(1, size)]
                self.tosend[i, rows] = sum(w * x for w, x in zip(total, pieces))
                prefix.append((pre, pieces))
            for dz in reversed(range(1, self.groups)):
                @pl.when(self.zl < self.groups - dz)
                def _():
                    self.b_copy(dz, c).start()
            for i in range(hp):
                pre, pieces = prefix[i]
                for off in range(size):
                    self.local[off, i, rows] = sum(w * x for w, x in zip(pre[off], pieces))
        for c in range(CHUNKS):
            rows = self.rows[c]
            for dz in range(1, self.groups):
                @pl.when(self.zl >= dz)
                def _():
                    self.b_copy(dz, c).wait_recv()
                    for i in range(hp):
                        self.fromprev[i, rows] += coef[i][3][dz - 1] * self.arrive[dz - 1, i, rows]
            for off in reversed(range(size)):
                for i in range(hp):
                    value = coef[i][2][off] * self.fromprev[i, rows] + self.local[off, i, rows]
                    if off:
                        self.back[off - 1, i, rows] = value
                    else:
                        self.whole[pl.ds(first + i, 1), rows] = value[None]
                if off:
                    self.c_copy(off, c).start()

    def finish(self):
        for c in range(CHUNKS):
            for off in range(1, self.size):
                self.c_copy(off, c).wait_recv()
                owner = lax.rem(self.rank + self.size - off, self.size)
                self.whole[pl.ds(owner * self.hp, self.hp), self.rows[c]] = self.landed[off - 1, :, self.rows[c]]

    def drain(self):
        for c in range(CHUNKS):
            for off in range(1, self.size):
                self.a_copy(off, c).wait_send()
                self.c_copy(off, c).wait_send()

            for dz in range(1, self.groups):
                @pl.when(self.zl < self.groups - dz)
                def _():
                    self.b_copy(dz, c).wait_send()


def scan_scratch(size, groups, hp, heads):
    state = lambda *lead: pltpu.VMEM(lead + (128, 128), F32)
    pair = pltpu.SemaphoreType.DMA((max(size - 1, 1), CHUNKS))
    jump = pltpu.SemaphoreType.DMA((max(groups - 1, 1), CHUNKS))
    peers = max(size - 1, 1)
    return [state(peers, hp), state(hp), state(max(groups - 1, 1), hp), state(hp), state(size, hp),
            state(peers, hp), state(peers, hp), pair, pair, jump, jump, pair, pair]


def kernel(n, m, groups, heads, rates_hbm, q_hbm, k_hbm, v_hbm, gain_hbm, og_hbm,
           normed_ref, qg_ref, kacc_ref, vacc_ref, k_ref, v_ref, backlog_ref, last_ref, rate_ref,
           rates, q_ref, og_ref, gain_ref, load_sem,
           w_ref, p_ref, x_ref, do_ref, first_ref, mine_ref, theirs_ref, h_send, h_recv, memory_ref, fparts, bparts,
           *scans):
    loads = [pltpu.make_async_copy(src, dst, load_sem.at[i]) for i, (src, dst) in enumerate(
        ((rates_hbm, rates), (k_hbm, k_ref), (v_hbm, v_ref), (q_hbm, q_ref), (og_hbm, og_ref), (gain_hbm, gain_ref)))]
    for load in loads:
        load.start()
    tokens = q_ref.shape[0]
    blocks = tokens // BLOCK
    size = n // groups
    hp = heads // size
    me, head = lax.axis_index("ctx"), lax.axis_index("head")
    half = len(scans) // 2
    make = functools.partial(Scan, n=n, groups=groups, hp=hp, length=tokens, rates=rates)
    names = ("got", "tosend", "arrive", "fromprev", "local", "back", "landed",
             "a_send", "a_recv", "b_send", "b_recv", "c_send", "c_recv")
    forward = make(reverse=False, parts=fparts, whole=memory_ref, **dict(zip(names, scans[:half])))
    backward = make(reverse=True, parts=bparts, whole=backlog_ref, **dict(zip(names, scans[half:])))

    barrier = pltpu.get_barrier_semaphore()
    for off in range(1, size):
        pl.semaphore_signal(barrier, inc=1, device_id={"ctx": forward.device(lax.rem(forward.rank + off, size))},
                            device_id_type=MESH)
    for off in range(1, m):
        pl.semaphore_signal(barrier, inc=1, device_id={"head": lax.rem(head + off, m)}, device_id_type=MESH)

    for off in range(1, groups):
        pl.semaphore_signal(barrier, inc=1, device_id={"ctx": lax.rem(me + off * size, n)}, device_id_type=MESH)

    position = lax.broadcasted_iota(jnp.int32, (BLOCK, 128), 0).astype(F32)

    def at(ref, b, h):
        return ref[b * BLOCK:(b + 1) * BLOCK, h * 128:(h + 1) * 128]

    for load in loads[:3]:
        load.wait()
    pl.semaphore_wait(barrier, size - 1 + m - 1 + groups - 1)

    for h in range(heads):
        trailing = jnp.exp(-rates[h] * (BLOCK - 1.0 - position))
        full = power(rates[h], float(BLOCK))
        state = None
        for b in range(blocks):
            high, low = split(at(k_ref, b, h).astype(F32) * trailing)
            v = at(v_ref, b, h)
            update = dot(high, v, 0, 0) + dot(low, v, 0, 0)
            if b < blocks - 1:
                first_ref[b, h] = update
            state = update if state is None else full * state + update
        forward.parts[h] = state
        forward.begin(h)

    for load in loads[3:]:
        load.wait()

    spacing = (lax.broadcasted_iota(jnp.int32, (BLOCK, BLOCK), 0)
               - lax.broadcasted_iota(jnp.int32, (BLOCK, BLOCK), 1))
    causal = spacing >= 0
    gap = jnp.maximum(spacing, 0).astype(F32)
    for h in range(heads):
        w = jnp.where(causal, jnp.exp(-rates[h] * gap), 0.0)
        w_ref[h] = w
        for b in range(blocks):
            p = (dot(at(q_ref, b, h), at(k_ref, b, h), 1, 1) * w).astype(BF16)
            p_ref[b, h] = p
            x_ref[b * BLOCK:(b + 1) * BLOCK, h * 128:(h + 1) * 128] = dot(p, at(v_ref, b, h), 1, 0)

    forward.relay()
    forward.finish()

    squares = [0.0] * blocks
    projection = [0.0] * blocks
    for h in range(heads):
        leading = jnp.exp(-rates[h] * (position + 1.0))
        full = power(rates[h], float(BLOCK))
        memory = forward.whole[h]
        gain = gain_ref[:, h * 128:(h + 1) * 128]
        for b in range(blocks):
            high, low = split(memory)
            q = at(q_ref, b, h)
            x = at(x_ref, b, h) + (dot(q, high, 1, 0) + dot(q, low, 1, 0)) * leading
            x_ref[b * BLOCK:(b + 1) * BLOCK, h * 128:(h + 1) * 128] = x
            squares[b] = squares[b] + x * x
            projection[b] = projection[b] + at(og_ref, b, h).astype(F32) * gain * x
            if b < blocks - 1:
                memory = full * memory + first_ref[b, h]

    lane = lax.broadcasted_iota(jnp.int32, (BLOCK, 128), 1)
    for b in range(blocks):
        pair = jnp.where(lane == 0, jnp.sum(squares[b], axis=1, keepdims=True),
                         jnp.sum(projection[b], axis=1, keepdims=True))
        mine_ref[:, b * BLOCK:(b + 1) * BLOCK] = pair.T[:8]

    def h_copy(off):
        return pltpu.make_async_remote_copy(
            src_ref=mine_ref, dst_ref=theirs_ref.at[off - 1], send_sem=h_send.at[off - 1],
            recv_sem=h_recv.at[off - 1], device_id={"head": lax.rem(head + off, m)}, device_id_type=MESH)

    for off in range(1, m):
        h_copy(off).start()
    for off in range(1, m):
        h_copy(off).wait_recv()
    sums = mine_ref[...]
    for off in range(1, m):
        sums = sums + theirs_ref[off - 1]
    features = float(heads * 128 * m)
    scale_row = lax.rsqrt(sums[0:1] / features + EPSILON)
    coeff_row = scale_row * sums[1:2] / features
    even = lax.broadcasted_iota(jnp.int32, (128, BLOCK), 0) == 0
    for b in range(blocks):
        cut = slice(b * BLOCK, (b + 1) * BLOCK)
        both = jnp.where(even, scale_row[:, cut], coeff_row[:, cut]).T
        scale = jnp.broadcast_to(both[:, 0:1], (BLOCK, 128))
        coeff = jnp.broadcast_to(both[:, 1:2], (BLOCK, 128))
        for h in range(heads):
            cols = slice(h * 128, (h + 1) * 128)
            gain = gain_ref[:, cols]
            normed = x_ref[cut, cols] * scale
            x_ref[cut, cols] = normed
            g = at(og_ref, b, h).astype(F32) * gain
            do_ref[cut, cols] = (scale * (g - normed * coeff)).astype(BF16)

    for h in range(heads):
        start = jnp.exp(-rates[h] * position)
        full = power(rates[h], float(BLOCK))
        state = None
        for b in reversed(range(blocks)):
            high, low = split(at(q_ref, b, h).astype(F32) * start)
            do = at(do_ref, b, h)
            update = dot(high, do, 0, 0) + dot(low, do, 0, 0)
            if b > 0:
                last_ref[b - 1, h] = update
            state = update if state is None else full * state + update
        backward.parts[h] = state
        backward.begin(h)

    for h in range(heads):
        leading = jnp.exp(-rates[h] * (position + 1.0))
        full = power(rates[h], float(BLOCK))
        memory = forward.whole[h]
        w = w_ref[h]
        cols = slice(h * 128, (h + 1) * 128)
        for b in range(blocks):
            cut = slice(b * BLOCK, (b + 1) * BLOCK)
            high, low = split(memory)
            normed_ref[cut, cols] = (x_ref[cut, cols] * gain_ref[:, cols]).astype(BF16)
            do, k, q = at(do_ref, b, h), at(k_ref, b, h), at(q_ref, b, h)
            s = (dot(do, at(v_ref, b, h), 1, 1) * w).astype(BF16)
            qg_ref[cut, cols] = (dot(s, k, 1, 0)
                                 + (dot(do, high, 1, 1) + dot(do, low, 1, 1)) * leading).astype(BF16)
            kacc_ref[cut, cols] = dot(s, q, 0, 0)
            vacc_ref[cut, cols] = dot(p_ref[b, h], do, 0, 0)
            if b < blocks - 1:
                memory = full * memory + first_ref[b, h]

    for h in range(heads):
        rate_ref[h] = jnp.full((8, 128), rates[h], F32)
    backward.relay()
    backward.finish()

    for off in range(1, m):
        h_copy(off).wait_send()
    forward.drain()
    backward.drain()


def last_kernel(heads, normed_ref, qg_ref, kacc_ref, vacc_ref, k_ref, v_ref, backlog_ref, last_ref, rate_ref,
                normed_hbm, qg_hbm, kg_hbm, vg_hbm, kg_ref, vg_ref, early_sem, late_sem):
    tokens = k_ref.shape[0]
    blocks = tokens // BLOCK
    early = [pltpu.make_async_copy(src, dst, early_sem.at[i])
             for i, (src, dst) in enumerate(((normed_ref, normed_hbm), (qg_ref, qg_hbm)))]
    for copy in early:
        copy.start()
    position = lax.broadcasted_iota(jnp.int32, (BLOCK, 128), 0).astype(F32)
    late = []
    for h in range(heads):
        rate = rate_ref[h, 0:1]
        after = jnp.exp(-rate * (BLOCK - position))
        full = jnp.exp(-rate * float(BLOCK))
        backlog = backlog_ref[h]
        cols = slice(h * 128, (h + 1) * 128)
        for b in reversed(range(blocks)):
            cut = slice(b * BLOCK, (b + 1) * BLOCK)
            high, low = split(backlog)
            v, k = v_ref[cut, cols], k_ref[cut, cols]
            kg_ref[cut, cols] = (kacc_ref[cut, cols]
                                 + (dot(v, high, 1, 1) + dot(v, low, 1, 1)) * after).astype(BF16)
            vg_ref[cut, cols] = (vacc_ref[cut, cols]
                                 + (dot(k, high, 1, 0) + dot(k, low, 1, 0)) * after).astype(BF16)
            if b > 0:
                backlog = full * backlog + last_ref[b - 1, h]
        for i, (src, dst) in enumerate(((kg_ref, kg_hbm), (vg_ref, vg_hbm))):
            copy = pltpu.make_async_copy(src.at[:, cols], dst.at[:, cols], late_sem.at[i, h])
            copy.start()
            late.append(copy)
    for copy in early + late:
        copy.wait()


def solution(mesh):
    n, m = mesh.shape["ctx"], mesh.shape["head"]

    def on_device(queries, key_rows, value_rows, decay_rates, norm_gain, out_grad):
        tokens, width = queries.shape
        heads = decay_rates.shape[0]
        blocks = tokens // BLOCK
        size = math.gcd(heads, n)
        groups, hp = n // size, heads // size
        vmem = pl.BlockSpec(memory_space=pltpu.VMEM)
        hbm = pl.BlockSpec(memory_space=pltpu.HBM)
        shape = jax.ShapeDtypeStruct
        dma = pltpu.SemaphoreType.DMA
        row = (tokens, width)
        carry = (max(blocks - 1, 1), heads, 128, 128)
        kept = (shape(row, BF16), shape(row, BF16), shape(row, F32), shape(row, F32), shape(row, BF16),
                shape(row, BF16), shape((heads, 128, 128), F32), shape(carry, F32), shape((heads, 8, 128), F32))
        held = pl.pallas_call(
            functools.partial(kernel, n, m, groups, heads),
            out_shape=kept,
            in_specs=[hbm] * 6,
            out_specs=(vmem,) * 9,
            scratch_shapes=[
                pltpu.SMEM((heads,), F32), pltpu.VMEM(row, BF16), pltpu.VMEM(row, BF16), pltpu.VMEM((1, width), F32),
                dma((6,)),
                pltpu.VMEM((heads, BLOCK, BLOCK), F32),
                pltpu.VMEM((blocks, heads, BLOCK, BLOCK), BF16),
                pltpu.VMEM(row, F32),
                pltpu.VMEM(row, BF16),
                pltpu.VMEM(carry, F32),
                pltpu.VMEM((8, tokens), F32),
                pltpu.VMEM((max(m - 1, 1), 8, tokens), F32),
                dma((max(m - 1, 1),)), dma((max(m - 1, 1),)),
                pltpu.VMEM((heads, 128, 128), F32), pltpu.VMEM((heads, 128, 128), F32),
                pltpu.VMEM((heads, 128, 128), F32),
            ] + scan_scratch(size, groups, hp, heads) * 2,
            compiler_params=pltpu.CompilerParams(
                collective_id=0, has_side_effects=True, vmem_limit_bytes=32 * 2**20),
        )(*[pltpu.with_memory_space_constraint(x, pltpu.HBM) for x in (
            decay_rates, queries, key_rows, value_rows, norm_gain.reshape(1, width), out_grad)])
        return pl.pallas_call(
            functools.partial(last_kernel, heads),
            out_shape=(shape(row, BF16),) * 4,
            in_specs=[vmem] * 9,
            out_specs=(hbm,) * 4,
            scratch_shapes=[pltpu.VMEM(row, BF16), pltpu.VMEM(row, BF16), dma((2,)), dma((2, heads))],
            compiler_params=pltpu.CompilerParams(vmem_limit_bytes=16 * 2**20),
        )(*held)

    rows = P("ctx", "head")
    return jax.shard_map(
        on_device, mesh=mesh, in_specs=(rows, rows, rows, P("head"), P("head"), rows),
        out_specs=(rows,) * 4, check_vma=False)
```

```python
import functools
import math

import jax
import jax.numpy as jnp
from jax import lax
from jax.experimental import pallas as pl
from jax.experimental.pallas import tpu as pltpu
from jax.sharding import PartitionSpec as P

BLOCK = 256
CHUNKS = 2
EPSILON = 1e-06
MESH = pl.DeviceIdType.MESH
F32 = jnp.float32
BF16 = jnp.bfloat16


def dot(a, b, ca, cb):
    return lax.dot_general(a, b, (((ca,), (cb,)), ((), ())), preferred_element_type=F32)


def split(a):
    high = a.astype(BF16)
    return high, (a - high.astype(F32)).astype(BF16)


def power(rate, count):
    return jnp.exp(jnp.full((1, 128), -rate * count, F32))


def partner(rank, off):
    bit = 1
    while bit <= off:
        if off & bit:
            rank = rank + bit - 2 * bit * lax.rem(rank // bit, 2)
        bit *= 2
    return rank


class Scan:
    def __init__(self, reverse, n, groups, hp, length, rates, parts, whole, got, tosend, arrive, fromprev, local,
                 back, landed, a_send, a_recv, b_send, b_recv, c_send, c_recv):
        self.reverse, self.n, self.hp, self.length = reverse, n, hp, length
        self.size, self.groups = n // groups, groups
        self.rates, self.parts, self.whole = rates, parts, whole
        self.got, self.tosend, self.arrive, self.fromprev = got, tosend, arrive, fromprev
        self.local, self.back, self.landed = local, back, landed
        self.sems = (a_send, a_recv, b_send, b_recv, c_send, c_recv)
        me = lax.axis_index("ctx")
        self.z = me // self.size
        r = me - self.z * self.size
        self.base = self.z * self.size
        self.rank = self.size - 1 - r if reverse else r
        self.zl = groups - 1 - self.z if reverse else self.z
        self.me = me
        self.rows = [pl.ds(c * (128 // CHUNKS), 128 // CHUNKS) for c in range(CHUNKS)]

    def device(self, rank):
        return self.base + (self.size - 1 - rank if self.reverse else rank)

    def a_copy(self, off, c, t=None):
        t = partner(self.rank, off) if t is None else t
        return pltpu.make_async_remote_copy(
            src_ref=self.parts.at[pl.ds(t * self.hp, self.hp), self.rows[c]],
            dst_ref=self.got.at[off - 1, :, self.rows[c]],
            send_sem=self.sems[0].at[off - 1, c], recv_sem=self.sems[1].at[off - 1, c],
            device_id={"ctx": self.device(t)}, device_id_type=MESH)

    def b_copy(self, dz, c):
        step = dz * self.size
        return pltpu.make_async_remote_copy(
            src_ref=self.tosend.at[:, self.rows[c]], dst_ref=self.arrive.at[dz - 1, :, self.rows[c]],
            send_sem=self.sems[2].at[dz - 1, c], recv_sem=self.sems[3].at[dz - 1, c],
            device_id={"ctx": self.me - step if self.reverse else self.me + step}, device_id_type=MESH)

    def c_copy(self, off, c):
        t = partner(self.rank, off)
        return pltpu.make_async_remote_copy(
            src_ref=self.back.at[off - 1, :, self.rows[c]], dst_ref=self.landed.at[off - 1, :, self.rows[c]],
            send_sem=self.sems[4].at[off - 1, c], recv_sem=self.sems[5].at[off - 1, c],
            device_id={"ctx": self.device(t)}, device_id_type=MESH)

    def begin(self, h):
        if (h + 1) % self.hp:
            return
        owner = h // self.hp
        off = sum(bit * lax.rem(self.rank // bit + owner // bit, 2)
                  for bit in (2 ** e for e in range(self.size.bit_length() - 1)))

        @pl.when(off > 0)
        def _():
            for c in range(CHUNKS):
                self.a_copy(off, c, owner).start()

    def relay(self):
        size, hp = self.size, self.hp
        first = self.rank * hp
        source = target = [partner(self.rank, off) for off in range(size)]
        coef = []
        for i in range(hp):
            step = self.rates[first + i] * float(self.length)
            total = [power(step, (size - 1 - e).astype(F32)) for e in source]
            pre = [[jnp.where(e < t, power(step, jnp.maximum(t - 1 - e, 0).astype(F32)), 0.0) for e in source]
                   for t in target]
            lead = [power(step, t.astype(F32)) for t in target]
            jump = [power(step, float(size * dz)) for dz in range(self.groups - 1)]
            coef.append((total, pre, lead, jump))
        self.fromprev[...] = jnp.zeros_like(self.fromprev)
        prefixes = []
        for c in range(CHUNKS):
            rows = self.rows[c]
            for off in range(1, size):
                self.a_copy(off, c).wait_recv()
            prefix = []
            for i in range(hp):
                total, pre, _, _ = coef[i]
                pieces = [self.parts[pl.ds(first + i, 1), rows][0]]
                pieces += [self.got[off - 1, i, rows] for off in range(1, size)]
                self.tosend[i, rows] = sum(w * x for w, x in zip(total, pieces))
                prefix.append((pre, pieces))
            for dz in reversed(range(1, self.groups)):
                @pl.when(self.zl < self.groups - dz)
                def _():
                    self.b_copy(dz, c).start()
            for i in range(hp):
                pre, pieces = prefix[i]
                for off in range(size):
                    self.local[off, i, rows] = sum(w * x for w, x in zip(pre[off], pieces))
        for c in range(CHUNKS):
            rows = self.rows[c]
            for dz in range(1, self.groups):
                @pl.when(self.zl >= dz)
                def _():
                    self.b_copy(dz, c).wait_recv()
                    for i in range(hp):
                        self.fromprev[i, rows] += coef[i][3][dz - 1] * self.arrive[dz - 1, i, rows]
            for off in reversed(range(size)):
                for i in range(hp):
                    value = coef[i][2][off] * self.fromprev[i, rows] + self.local[off, i, rows]
                    if off:
                        self.back[off - 1, i, rows] = value
                    else:
                        self.whole[pl.ds(first + i, 1), rows] = value[None]
                if off:
                    self.c_copy(off, c).start()

    def finish(self, off):
        owner = partner(self.rank, off)
        if off:
            for c in range(CHUNKS):
                self.c_copy(off, c).wait_recv()
            self.whole[pl.ds(owner * self.hp, self.hp)] = self.landed[off - 1]
        return owner

    def drain(self):
        for c in range(CHUNKS):
            for off in range(1, self.size):
                self.a_copy(off, c).wait_send()
                self.c_copy(off, c).wait_send()

            for dz in range(1, self.groups):
                @pl.when(self.zl < self.groups - dz)
                def _():
                    self.b_copy(dz, c).wait_send()


def scan_scratch(size, groups, hp, heads):
    state = lambda *lead: pltpu.VMEM(lead + (128, 128), F32)
    pair = pltpu.SemaphoreType.DMA((max(size - 1, 1), CHUNKS))
    jump = pltpu.SemaphoreType.DMA((max(groups - 1, 1), CHUNKS))
    peers = max(size - 1, 1)
    return [state(peers, hp), state(hp), state(max(groups - 1, 1), hp), state(hp), state(size, hp),
            state(peers, hp), state(peers, hp), pair, pair, jump, jump, pair, pair]


def kernel(n, m, groups, heads, rates_hbm, q_hbm, k_hbm, v_hbm, gain_hbm, og_hbm,
           normed_ref, qg_ref, kacc_ref, vacc_ref, k_ref, v_ref, backlog_ref, last_ref, rate_ref, after_ref,
           rates, q_ref, og_ref, gain_ref, load_sem,
           w_ref, p_ref, x_ref, do_ref, g_ref, turned_ref, lead_ref, first_ref, mine_ref, theirs_ref, h_send, h_recv, memory_ref, fparts, bparts,
           *scans):
    loads = [pltpu.make_async_copy(src, dst, load_sem.at[i]) for i, (src, dst) in enumerate(
        ((rates_hbm, rates), (k_hbm, k_ref), (v_hbm, v_ref), (q_hbm, q_ref), (og_hbm, og_ref), (gain_hbm, gain_ref)))]
    for load in loads:
        load.start()
    tokens = q_ref.shape[0]
    blocks = tokens // BLOCK
    size = n // groups
    hp = heads // size
    me, head = lax.axis_index("ctx"), lax.axis_index("head")
    half = len(scans) // 2
    make = functools.partial(Scan, n=n, groups=groups, hp=hp, length=tokens, rates=rates)
    names = ("got", "tosend", "arrive", "fromprev", "local", "back", "landed",
             "a_send", "a_recv", "b_send", "b_recv", "c_send", "c_recv")
    forward = make(reverse=False, parts=fparts, whole=memory_ref, **dict(zip(names, scans[:half])))
    backward = make(reverse=True, parts=bparts, whole=backlog_ref, **dict(zip(names, scans[half:])))

    barrier = pltpu.get_barrier_semaphore()
    for off in range(1, size):
        pl.semaphore_signal(barrier, inc=1, device_id={"ctx": forward.device(partner(forward.rank, off))},
                            device_id_type=MESH)
    for off in range(1, m):
        pl.semaphore_signal(barrier, inc=1, device_id={"head": lax.rem(head + off, m)}, device_id_type=MESH)

    for off in range(1, groups):
        pl.semaphore_signal(barrier, inc=1, device_id={"ctx": lax.rem(me + off * size, n)}, device_id_type=MESH)

    position = lax.broadcasted_iota(jnp.int32, (BLOCK, 128), 0).astype(F32)

    def at(ref, b, h):
        return ref[b * BLOCK:(b + 1) * BLOCK, h * 128:(h + 1) * 128]

    for load in loads[:3]:
        load.wait()
    pl.semaphore_wait(barrier, size - 1 + m - 1 + groups - 1)

    for h in range(heads):
        trailing = jnp.exp(-rates[h] * (BLOCK - 1.0 - position))
        full = power(rates[h], float(BLOCK))
        state = None
        for b in range(blocks):
            scaled = jnp.concatenate(split(at(v_ref, b, h).astype(F32) * trailing), axis=1)
            both = dot(at(k_ref, b, h), scaled, 0, 0)
            update = both[:, :128] + both[:, 128:]
            if b < blocks - 1:
                first_ref[b, h] = update
            state = update if state is None else full * state + update
        forward.parts[h] = state
        forward.begin(h)

    for load in loads[3:]:
        load.wait()

    spacing = (lax.broadcasted_iota(jnp.int32, (BLOCK, BLOCK), 0)
               - lax.broadcasted_iota(jnp.int32, (BLOCK, BLOCK), 1))
    causal = spacing >= 0
    gap = jnp.maximum(spacing, 0).astype(F32)
    for h in range(heads):
        w = jnp.where(causal, jnp.exp(-rates[h] * gap), 0.0)
        w_ref[h] = w
        lead_ref[h] = jnp.exp(-rates[h] * (position + 1.0))
        after_ref[h] = jnp.exp(-rates[h] * (BLOCK - position))
        rate_ref[h] = jnp.full((8, 128), rates[h], F32)
        start = jnp.exp(-rates[h] * position)
        cols = slice(h * 128, (h + 1) * 128)
        gain = gain_ref[:, cols]
        for b in range(blocks):
            p = (dot(at(q_ref, b, h), at(k_ref, b, h), 1, 1) * w).astype(BF16)
            p_ref[b, h] = p
            x_ref[b * BLOCK:(b + 1) * BLOCK, h * 128:(h + 1) * 128] = dot(p, at(v_ref, b, h), 1, 0)
            cut = slice(b * BLOCK, (b + 1) * BLOCK)
            g_ref[cut, cols] = at(og_ref, b, h).astype(F32) * gain
            turned = (at(q_ref, b, h).astype(F32) * start).T
            turned_ref[b, h] = jnp.concatenate(split(turned), axis=1)

    forward.relay()

    squares = [0.0] * blocks
    projection = [0.0] * blocks
    for off in range(size):
        owner = forward.finish(off)
        for i in range(hp):
            h = owner * hp + i
            cols = pl.ds(pl.multiple_of(h * 128, 128), 128)
            full = power(rates[h], float(BLOCK))
            memory = memory_ref[h]
            for b in range(blocks):
                cut = slice(b * BLOCK, (b + 1) * BLOCK)
                q = q_ref[cut, cols]
                carried = dot(jnp.concatenate([q, q], axis=1), jnp.concatenate(split(memory), axis=0), 1, 0)
                x = x_ref[cut, cols] + carried * lead_ref[h]
                x_ref[cut, cols] = x
                squares[b] = squares[b] + x * x
                projection[b] = projection[b] + g_ref[cut, cols] * x
                if b < blocks - 1:
                    memory = full * memory + first_ref[b, h]

    lane = lax.broadcasted_iota(jnp.int32, (BLOCK, 128), 1)
    for b in range(blocks):
        pair = jnp.where(lane == 0, jnp.sum(squares[b], axis=1, keepdims=True),
                         jnp.sum(projection[b], axis=1, keepdims=True))
        mine_ref[:, b * BLOCK:(b + 1) * BLOCK] = pair.T[:8]

    def h_copy(off):
        return pltpu.make_async_remote_copy(
            src_ref=mine_ref, dst_ref=theirs_ref.at[off - 1], send_sem=h_send.at[off - 1],
            recv_sem=h_recv.at[off - 1], device_id={"head": lax.rem(head + off, m)}, device_id_type=MESH)

    for off in range(1, m):
        h_copy(off).start()
    for off in range(1, m):
        h_copy(off).wait_recv()
    sums = mine_ref[...]
    for off in range(1, m):
        sums = sums + theirs_ref[off - 1]
    features = float(heads * 128 * m)
    scale_row = lax.rsqrt(sums[0:1] / features + EPSILON)
    coeff_row = scale_row * sums[1:2] / features
    even = lax.broadcasted_iota(jnp.int32, (128, BLOCK), 0) == 0
    for b in range(blocks):
        cut = slice(b * BLOCK, (b + 1) * BLOCK)
        both = jnp.where(even, scale_row[:, cut], coeff_row[:, cut]).T
        scale = jnp.broadcast_to(both[:, 0:1], (BLOCK, 128))
        coeff = jnp.broadcast_to(both[:, 1:2], (BLOCK, 128))
        for h in range(heads):
            cols = slice(h * 128, (h + 1) * 128)
            normed = x_ref[cut, cols] * scale
            x_ref[cut, cols] = normed
            do_ref[cut, cols] = (scale * (g_ref[cut, cols] - normed * coeff)).astype(BF16)

    for h in range(heads):
        full = power(rates[h], float(BLOCK))
        state = None
        for b in reversed(range(blocks)):
            do = at(do_ref, b, h)
            update = dot(turned_ref[b, h], jnp.concatenate([do, do], axis=0), 1, 0)
            if b > 0:
                last_ref[b - 1, h] = update
            state = update if state is None else full * state + update
        backward.parts[h] = state
        backward.begin(h)

    for h in range(heads):
        full = power(rates[h], float(BLOCK))
        memory = memory_ref[h]
        w = w_ref[h]
        cols = slice(h * 128, (h + 1) * 128)
        for b in range(blocks):
            cut = slice(b * BLOCK, (b + 1) * BLOCK)
            normed_ref[cut, cols] = (x_ref[cut, cols] * gain_ref[:, cols]).astype(BF16)
            do, k, q = at(do_ref, b, h), at(k_ref, b, h), at(q_ref, b, h)
            s = (dot(do, at(v_ref, b, h), 1, 1) * w).astype(BF16)
            qg_ref[cut, cols] = (dot(s, k, 1, 0)
                                 + dot(jnp.concatenate([do, do], axis=1), jnp.concatenate(split(memory), axis=1), 1, 1)
                                 * lead_ref[h]).astype(BF16)
            kacc_ref[cut, cols] = dot(s, q, 0, 0)
            vacc_ref[cut, cols] = dot(p_ref[b, h], do, 0, 0)
            if b < blocks - 1:
                memory = full * memory + first_ref[b, h]

    backward.relay()
    for off in range(size):
        backward.finish(off)

    for off in range(1, m):
        h_copy(off).wait_send()
    forward.drain()
    backward.drain()


def last_kernel(heads, normed_ref, qg_ref, kacc_ref, vacc_ref, k_ref, v_ref, backlog_ref, last_ref, rate_ref,
                after_ref, normed_hbm, qg_hbm, kg_hbm, vg_hbm, kg_ref, vg_ref, early_sem, late_sem):
    tokens = k_ref.shape[0]
    blocks = tokens // BLOCK
    early = [pltpu.make_async_copy(src, dst, early_sem.at[i])
             for i, (src, dst) in enumerate(((normed_ref, normed_hbm), (qg_ref, qg_hbm)))]
    for copy in early:
        copy.start()
    late = []
    for h in range(heads):
        rate = rate_ref[h, 0:1]
        after = after_ref[h]
        full = jnp.exp(-rate * float(BLOCK))
        backlog = backlog_ref[h]
        cols = slice(h * 128, (h + 1) * 128)
        for b in reversed(range(blocks)):
            cut = slice(b * BLOCK, (b + 1) * BLOCK)
            pair = split(backlog)
            v, k = v_ref[cut, cols], k_ref[cut, cols]
            key_part = dot(jnp.concatenate([v, v], axis=1), jnp.concatenate(pair, axis=1), 1, 1)
            value_part = dot(jnp.concatenate([k, k], axis=1), jnp.concatenate(pair, axis=0), 1, 0)
            kg_ref[cut, cols] = (kacc_ref[cut, cols] + key_part * after).astype(BF16)
            vg_ref[cut, cols] = (vacc_ref[cut, cols] + value_part * after).astype(BF16)
            if b > 0:
                backlog = full * backlog + last_ref[b - 1, h]
        for i, (src, dst) in enumerate(((kg_ref, kg_hbm), (vg_ref, vg_hbm))):
            copy = pltpu.make_async_copy(src.at[:, cols], dst.at[:, cols], late_sem.at[i, h])
            copy.start()
            late.append(copy)
    for copy in early + late:
        copy.wait()


def solution(mesh):
    n, m = mesh.shape["ctx"], mesh.shape["head"]

    def on_device(queries, key_rows, value_rows, decay_rates, norm_gain, out_grad):
        tokens, width = queries.shape
        heads = decay_rates.shape[0]
        blocks = tokens // BLOCK
        size = math.gcd(heads, n)
        size = size & -size
        groups, hp = n // size, heads // size
        vmem = pl.BlockSpec(memory_space=pltpu.VMEM)
        hbm = pl.BlockSpec(memory_space=pltpu.HBM)
        shape = jax.ShapeDtypeStruct
        dma = pltpu.SemaphoreType.DMA
        row = (tokens, width)
        carry = (max(blocks - 1, 1), heads, 128, 128)
        kept = (shape(row, BF16), shape(row, BF16), shape(row, F32), shape(row, F32), shape(row, BF16),
                shape(row, BF16), shape((heads, 128, 128), F32), shape(carry, F32), shape((heads, 8, 128), F32),
                shape((heads, BLOCK, 128), F32))
        held = pl.pallas_call(
            functools.partial(kernel, n, m, groups, heads),
            out_shape=kept,
            in_specs=[hbm] * 6,
            out_specs=(vmem,) * 10,
            scratch_shapes=[
                pltpu.SMEM((heads,), F32), pltpu.VMEM(row, BF16), pltpu.VMEM(row, BF16), pltpu.VMEM((1, width), F32),
                dma((6,)),
                pltpu.VMEM((heads, BLOCK, BLOCK), F32),
                pltpu.VMEM((blocks, heads, BLOCK, BLOCK), BF16),
                pltpu.VMEM(row, F32),
                pltpu.VMEM(row, BF16),
                pltpu.VMEM(row, F32),
                pltpu.VMEM((blocks, heads, 128, 2 * BLOCK), BF16),
                pltpu.VMEM((heads, BLOCK, 128), F32),
                pltpu.VMEM(carry, F32),
                pltpu.VMEM((8, tokens), F32),
                pltpu.VMEM((max(m - 1, 1), 8, tokens), F32),
                dma((max(m - 1, 1),)), dma((max(m - 1, 1),)),
                pltpu.VMEM((heads, 128, 128), F32), pltpu.VMEM((heads, 128, 128), F32),
                pltpu.VMEM((heads, 128, 128), F32),
            ] + scan_scratch(size, groups, hp, heads) * 2,
            compiler_params=pltpu.CompilerParams(
                collective_id=0, has_side_effects=True, vmem_limit_bytes=32 * 2**20),
        )(*[pltpu.with_memory_space_constraint(x, pltpu.HBM) for x in (
            decay_rates, queries, key_rows, value_rows, norm_gain.reshape(1, width), out_grad)])
        return pl.pallas_call(
            functools.partial(last_kernel, heads),
            out_shape=(shape(row, BF16),) * 4,
            in_specs=[vmem] * 10,
            out_specs=(hbm,) * 4,
            scratch_shapes=[pltpu.VMEM(row, BF16), pltpu.VMEM(row, BF16), dma((2,)), dma((2, heads))],
            compiler_params=pltpu.CompilerParams(vmem_limit_bytes=16 * 2**20),
        )(*held)

    rows = P("ctx", "head")
    return jax.shard_map(
        on_device, mesh=mesh, in_specs=(rows, rows, rows, P("head"), P("head"), rows),
        out_specs=(rows,) * 4, check_vma=False)
```

```python
import functools
import math

import jax
import jax.numpy as jnp
from jax import lax
from jax.experimental import pallas as pl
from jax.experimental.pallas import tpu as pltpu
from jax.sharding import PartitionSpec as P

BLOCK = 256
CHUNKS = 2
PIECES = 2
EPSILON = 1e-06
MESH = pl.DeviceIdType.MESH
F32 = jnp.float32
BF16 = jnp.bfloat16


def dot(a, b, ca, cb):
    return lax.dot_general(a, b, (((ca,), (cb,)), ((), ())), preferred_element_type=F32)


def split(a):
    high = a.astype(BF16)
    return high, (a - high.astype(F32)).astype(BF16)


def power(rate, count):
    return jnp.exp(jnp.full((1, 128), -rate * count, F32))


def partner(rank, off):
    bit = 1
    while bit <= off:
        if off & bit:
            rank = rank + bit - 2 * bit * lax.rem(rank // bit, 2)
        bit *= 2
    return rank


class Scan:
    def __init__(self, reverse, n, groups, hp, pieces, length, rates, parts, whole, got, tosend, arrive, fromprev,
                 back, a_send, a_recv, b_send, b_recv, c_send, c_recv):
        self.reverse, self.n, self.hp, self.pieces, self.length = reverse, n, hp, pieces, length
        self.size, self.groups = n // groups, groups
        self.rates, self.parts, self.whole = rates, parts, whole
        self.got, self.tosend, self.arrive, self.fromprev, self.back = got, tosend, arrive, fromprev, back
        self.sems = (a_send, a_recv, b_send, b_recv, c_send, c_recv)
        me = lax.axis_index("ctx")
        self.z = me // self.size
        r = me - self.z * self.size
        self.base = self.z * self.size
        self.rank = self.size - 1 - r if reverse else r
        self.zl = groups - 1 - self.z if reverse else self.z
        self.me = me
        self.height = 128 // pieces // CHUNKS
        self.rows = [pl.ds(c * self.height, self.height) for c in range(CHUNKS)]

    def device(self, rank):
        return self.base + (self.size - 1 - rank if self.reverse else rank)

    def share(self, rank):
        return pl.ds(rank * self.hp, self.hp)

    def a_copy(self, off, c, to, slot):
        return pltpu.make_async_remote_copy(
            src_ref=self.parts.at[self.share(to), self.rows[c]],
            dst_ref=self.got.at[slot, :, self.rows[c]],
            send_sem=self.sems[0].at[off - 1, c], recv_sem=self.sems[1].at[off - 1, c],
            device_id={"ctx": self.device(to)}, device_id_type=MESH)

    def b_copy(self, dz, c):
        step = dz * self.size
        return pltpu.make_async_remote_copy(
            src_ref=self.tosend.at[:, self.rows[c]], dst_ref=self.arrive.at[dz - 1, :, self.rows[c]],
            send_sem=self.sems[2].at[dz - 1, c], recv_sem=self.sems[3].at[dz - 1, c],
            device_id={"ctx": self.me - step if self.reverse else self.me + step}, device_id_type=MESH)

    def c_copy(self, off, c, owner):
        to = partner(self.rank, off)
        return pltpu.make_async_remote_copy(
            src_ref=self.back.at[to, :, self.rows[c]],
            dst_ref=self.whole.at[self.share(owner), self.rows[c]],
            send_sem=self.sems[4].at[off - 1, c], recv_sem=self.sems[5].at[off - 1, c],
            device_id={"ctx": self.device(to)}, device_id_type=MESH)

    def begin(self, h, state):
        tall = 128 // self.pieces
        for i in range(self.pieces):
            self.parts[h * self.pieces + i] = state[i * tall:(i + 1) * tall]
            if (h * self.pieces + i + 1) % self.hp:
                continue
            owner = (h * self.pieces + i) // self.hp
            off = sum(bit * lax.rem(self.rank // bit + owner // bit, 2)
                      for bit in (2 ** e for e in range(self.size.bit_length() - 1)))

            @pl.when(off > 0)
            def _():
                for c in range(CHUNKS):
                    self.a_copy(off, c, owner, self.rank).start()

    def relay(self):
        size, hp = self.size, self.hp
        first = self.rank * hp
        steps = [self.rates[(first + i) // self.pieces] * float(self.length) for i in range(hp)]
        powers = [[power(step, float(e)) for e in range(size + 1)] for step in steps]
        jumps = [[power(step, float(size * dz)) for dz in range(self.groups - 1)] for step in steps]
        self.got[pl.ds(self.rank, 1)] = self.parts[self.share(self.rank)][None]
        for c in range(CHUNKS):
            rows = self.rows[c]
            for off in range(1, size):
                peer = partner(self.rank, off)
                self.a_copy(off, c, peer, peer).wait_recv()
            for i in range(hp):
                run = self.got[0, i, rows]
                for e in range(1, size):
                    self.back[e, i, rows] = run
                    run = powers[i][1] * run + self.got[e, i, rows]
                self.tosend[i, rows] = run
            for dz in reversed(range(1, self.groups)):
                @pl.when(self.zl < self.groups - dz)
                def _():
                    self.b_copy(dz, c).start()
        self.fromprev[...] = jnp.zeros_like(self.fromprev)
        for c in range(CHUNKS):
            rows = self.rows[c]
            for dz in range(1, self.groups):
                @pl.when(self.zl >= dz)
                def _():
                    self.b_copy(dz, c).wait_recv()
                    for i in range(hp):
                        self.fromprev[i, rows] += jumps[i][dz - 1] * self.arrive[dz - 1, i, rows]
            for i in range(hp):
                before = self.fromprev[i, rows]
                self.back[0, i, rows] = before
                for e in range(1, size):
                    self.back[e, i, rows] += powers[i][e] * before
            for off in reversed(range(1, size)):
                self.c_copy(off, c, self.rank).start()
            self.whole[self.share(self.rank), rows] = self.back[pl.ds(self.rank, 1), :, rows][0]

    def finish(self, off):
        owner = partner(self.rank, off)
        if off:
            for c in range(CHUNKS):
                self.c_copy(off, c, owner).wait_recv()
        return owner

    def state(self, h):
        return self.whole[pl.ds(h * self.pieces, self.pieces)].reshape(128, 128)

    def drain(self):
        for c in range(CHUNKS):
            for off in range(1, self.size):
                peer = partner(self.rank, off)
                self.a_copy(off, c, peer, self.rank).wait_send()
                self.c_copy(off, c, self.rank).wait_send()
            for dz in range(1, self.groups):
                @pl.when(self.zl < self.groups - dz)
                def _():
                    self.b_copy(dz, c).wait_send()


def scan_scratch(size, groups, hp, pieces):
    state = lambda *lead: pltpu.VMEM(lead + (128 // pieces, 128), F32)
    pair = pltpu.SemaphoreType.DMA((max(size - 1, 1), CHUNKS))
    jump = pltpu.SemaphoreType.DMA((max(groups - 1, 1), CHUNKS))
    return [state(size, hp), state(hp), state(max(groups - 1, 1), hp), state(hp), state(size, hp),
            pair, pair, jump, jump, pair, pair]


def kernel(n, m, groups, heads, pieces, rates_hbm, q_hbm, k_hbm, v_hbm, gain_hbm, og_hbm,
           normed_ref, qg_ref, kacc_ref, vacc_ref, k_ref, v_ref, backlog_ref, last_ref, rate_ref, after_ref,
           rates, q_ref, og_ref, gain_ref, load_sem,
           w_ref, p_ref, x_ref, do_ref, g_ref, turned_ref, lead_ref, first_ref, mine_ref, theirs_ref, h_send, h_recv, memory_ref, fparts, bparts,
           *scans):
    loads = [pltpu.make_async_copy(src, dst, load_sem.at[i]) for i, (src, dst) in enumerate(
        ((rates_hbm, rates), (k_hbm, k_ref), (v_hbm, v_ref), (q_hbm, q_ref), (og_hbm, og_ref), (gain_hbm, gain_ref)))]
    for load in loads:
        load.start()
    tokens = q_ref.shape[0]
    blocks = tokens // BLOCK
    size = n // groups
    hp = heads * pieces // size
    me, head = lax.axis_index("ctx"), lax.axis_index("head")
    half = len(scans) // 2
    make = functools.partial(Scan, n=n, groups=groups, hp=hp, pieces=pieces, length=tokens, rates=rates)
    names = ("got", "tosend", "arrive", "fromprev", "back",
             "a_send", "a_recv", "b_send", "b_recv", "c_send", "c_recv")
    forward = make(reverse=False, parts=fparts, whole=memory_ref, **dict(zip(names, scans[:half])))
    backward = make(reverse=True, parts=bparts, whole=backlog_ref, **dict(zip(names, scans[half:])))

    barrier = pltpu.get_barrier_semaphore()
    for off in range(1, size):
        pl.semaphore_signal(barrier, inc=1, device_id={"ctx": forward.device(partner(forward.rank, off))},
                            device_id_type=MESH)
    for off in range(1, m):
        pl.semaphore_signal(barrier, inc=1, device_id={"head": lax.rem(head + off, m)}, device_id_type=MESH)

    for off in range(1, groups):
        pl.semaphore_signal(barrier, inc=1, device_id={"ctx": lax.rem(me + off * size, n)}, device_id_type=MESH)

    position = lax.broadcasted_iota(jnp.int32, (BLOCK, 128), 0).astype(F32)

    def at(ref, b, h):
        return ref[b * BLOCK:(b + 1) * BLOCK, h * 128:(h + 1) * 128]

    for load in loads[:3]:
        load.wait()
    pl.semaphore_wait(barrier, size - 1 + m - 1 + groups - 1)

    for h in range(heads):
        trailing = jnp.exp(-rates[h] * (BLOCK - 1.0 - position))
        full = power(rates[h], float(BLOCK))
        state = None
        for b in range(blocks):
            scaled = jnp.concatenate(split(at(v_ref, b, h).astype(F32) * trailing), axis=1)
            both = dot(at(k_ref, b, h), scaled, 0, 0)
            update = both[:, :128] + both[:, 128:]
            if b < blocks - 1:
                first_ref[b, h] = update
            state = update if state is None else full * state + update
        forward.begin(h, state)

    for load in loads[3:]:
        load.wait()

    spacing = (lax.broadcasted_iota(jnp.int32, (BLOCK, BLOCK), 0)
               - lax.broadcasted_iota(jnp.int32, (BLOCK, BLOCK), 1))
    causal = spacing >= 0
    gap = jnp.maximum(spacing, 0).astype(F32)
    for h in range(heads):
        w = jnp.where(causal, jnp.exp(-rates[h] * gap), 0.0)
        w_ref[h] = w
        lead_ref[h] = jnp.exp(-rates[h] * (position + 1.0))
        after_ref[h] = jnp.exp(-rates[h] * (BLOCK - position))
        rate_ref[h] = jnp.full((8, 128), rates[h], F32)
        start = jnp.exp(-rates[h] * position)
        cols = slice(h * 128, (h + 1) * 128)
        gain = gain_ref[:, cols]
        for b in range(blocks):
            p = (dot(at(q_ref, b, h), at(k_ref, b, h), 1, 1) * w).astype(BF16)
            p_ref[b, h] = p
            x_ref[b * BLOCK:(b + 1) * BLOCK, h * 128:(h + 1) * 128] = dot(p, at(v_ref, b, h), 1, 0)
            cut = slice(b * BLOCK, (b + 1) * BLOCK)
            g_ref[cut, cols] = at(og_ref, b, h).astype(F32) * gain
            turned = (at(q_ref, b, h).astype(F32) * start).T
            turned_ref[b, h] = jnp.concatenate(split(turned), axis=1)

    forward.relay()

    squares = [0.0] * blocks
    projection = [0.0] * blocks
    for first in range(0, size, pieces):
        owner = forward.finish(first)
        for off in range(first + 1, first + pieces):
            forward.finish(off)
        for i in range(max(hp // pieces, 1)):
            h = owner * hp // pieces + i
            cols = pl.ds(pl.multiple_of(h * 128, 128), 128)
            full = power(rates[h], float(BLOCK))
            memory = forward.state(h)
            for b in range(blocks):
                cut = slice(b * BLOCK, (b + 1) * BLOCK)
                q = q_ref[cut, cols]
                carried = dot(jnp.concatenate([q, q], axis=1), jnp.concatenate(split(memory), axis=0), 1, 0)
                x = x_ref[cut, cols] + carried * lead_ref[h]
                x_ref[cut, cols] = x
                squares[b] = squares[b] + x * x
                projection[b] = projection[b] + g_ref[cut, cols] * x
                if b < blocks - 1:
                    memory = full * memory + first_ref[b, h]

    lane = lax.broadcasted_iota(jnp.int32, (BLOCK, 128), 1)
    for b in range(blocks):
        pair = jnp.where(lane == 0, jnp.sum(squares[b], axis=1, keepdims=True),
                         jnp.sum(projection[b], axis=1, keepdims=True))
        mine_ref[:, b * BLOCK:(b + 1) * BLOCK] = pair.T[:8]

    def h_copy(off):
        return pltpu.make_async_remote_copy(
            src_ref=mine_ref, dst_ref=theirs_ref.at[off - 1], send_sem=h_send.at[off - 1],
            recv_sem=h_recv.at[off - 1], device_id={"head": lax.rem(head + off, m)}, device_id_type=MESH)

    for off in range(1, m):
        h_copy(off).start()
    for off in range(1, m):
        h_copy(off).wait_recv()
    sums = mine_ref[...]
    for off in range(1, m):
        sums = sums + theirs_ref[off - 1]
    features = float(heads * 128 * m)
    scale_row = lax.rsqrt(sums[0:1] / features + EPSILON)
    coeff_row = scale_row * sums[1:2] / features
    even = lax.broadcasted_iota(jnp.int32, (128, BLOCK), 0) == 0
    for b in range(blocks):
        cut = slice(b * BLOCK, (b + 1) * BLOCK)
        both = jnp.where(even, scale_row[:, cut], coeff_row[:, cut]).T
        scale = jnp.broadcast_to(both[:, 0:1], (BLOCK, 128))
        coeff = jnp.broadcast_to(both[:, 1:2], (BLOCK, 128))
        for h in range(heads):
            cols = slice(h * 128, (h + 1) * 128)
            normed = x_ref[cut, cols] * scale
            x_ref[cut, cols] = normed
            do_ref[cut, cols] = (scale * (g_ref[cut, cols] - normed * coeff)).astype(BF16)

    for h in range(heads):
        full = power(rates[h], float(BLOCK))
        state = None
        for b in reversed(range(blocks)):
            do = at(do_ref, b, h)
            update = dot(turned_ref[b, h], jnp.concatenate([do, do], axis=0), 1, 0)
            if b > 0:
                last_ref[b - 1, h] = update
            state = update if state is None else full * state + update
        backward.begin(h, state)

    for h in range(heads):
        full = power(rates[h], float(BLOCK))
        memory = forward.state(h)
        w = w_ref[h]
        cols = slice(h * 128, (h + 1) * 128)
        for b in range(blocks):
            cut = slice(b * BLOCK, (b + 1) * BLOCK)
            normed_ref[cut, cols] = (x_ref[cut, cols] * gain_ref[:, cols]).astype(BF16)
            do, k, q = at(do_ref, b, h), at(k_ref, b, h), at(q_ref, b, h)
            s = (dot(do, at(v_ref, b, h), 1, 1) * w).astype(BF16)
            qg_ref[cut, cols] = (dot(s, k, 1, 0)
                                 + dot(jnp.concatenate([do, do], axis=1), jnp.concatenate(split(memory), axis=1), 1, 1)
                                 * lead_ref[h]).astype(BF16)
            kacc_ref[cut, cols] = dot(s, q, 0, 0)
            vacc_ref[cut, cols] = dot(p_ref[b, h], do, 0, 0)
            if b < blocks - 1:
                memory = full * memory + first_ref[b, h]

    backward.relay()
    for off in range(size):
        backward.finish(off)

    for off in range(1, m):
        h_copy(off).wait_send()
    forward.drain()
    backward.drain()


def last_kernel(heads, normed_ref, qg_ref, kacc_ref, vacc_ref, k_ref, v_ref, backlog_ref, last_ref, rate_ref,
                after_ref, normed_hbm, qg_hbm, kg_hbm, vg_hbm, kg_ref, vg_ref, early_sem, late_sem):
    tokens = k_ref.shape[0]
    blocks = tokens // BLOCK
    early = [pltpu.make_async_copy(src, dst, early_sem.at[i])
             for i, (src, dst) in enumerate(((normed_ref, normed_hbm), (qg_ref, qg_hbm)))]
    for copy in early:
        copy.start()
    late = []
    for h in range(heads):
        rate = rate_ref[h, 0:1]
        after = after_ref[h]
        full = jnp.exp(-rate * float(BLOCK))
        pieces = backlog_ref.shape[0] // heads
        backlog = backlog_ref[h * pieces:(h + 1) * pieces].reshape(128, 128)
        cols = slice(h * 128, (h + 1) * 128)
        for b in reversed(range(blocks)):
            cut = slice(b * BLOCK, (b + 1) * BLOCK)
            pair = split(backlog)
            v, k = v_ref[cut, cols], k_ref[cut, cols]
            key_part = dot(jnp.concatenate([v, v], axis=1), jnp.concatenate(pair, axis=1), 1, 1)
            value_part = dot(jnp.concatenate([k, k], axis=1), jnp.concatenate(pair, axis=0), 1, 0)
            kg_ref[cut, cols] = (kacc_ref[cut, cols] + key_part * after).astype(BF16)
            vg_ref[cut, cols] = (vacc_ref[cut, cols] + value_part * after).astype(BF16)
            if b > 0:
                backlog = full * backlog + last_ref[b - 1, h]
        for i, (src, dst) in enumerate(((kg_ref, kg_hbm), (vg_ref, vg_hbm))):
            copy = pltpu.make_async_copy(src.at[:, cols], dst.at[:, cols], late_sem.at[i, h])
            copy.start()
            late.append(copy)
    for copy in early + late:
        copy.wait()


def solution(mesh):
    n, m = mesh.shape["ctx"], mesh.shape["head"]

    def on_device(queries, key_rows, value_rows, decay_rates, norm_gain, out_grad):
        tokens, width = queries.shape
        heads = decay_rates.shape[0]
        blocks = tokens // BLOCK
        size = math.gcd(heads * PIECES, n)
        size = size & -size
        pieces = max(size // (heads & -heads), 1)
        groups, hp = n // size, heads * pieces // size
        states = (heads * pieces, 128 // pieces, 128)
        vmem = pl.BlockSpec(memory_space=pltpu.VMEM)
        hbm = pl.BlockSpec(memory_space=pltpu.HBM)
        shape = jax.ShapeDtypeStruct
        dma = pltpu.SemaphoreType.DMA
        row = (tokens, width)
        carry = (max(blocks - 1, 1), heads, 128, 128)
        kept = (shape(row, BF16), shape(row, BF16), shape(row, F32), shape(row, F32), shape(row, BF16),
                shape(row, BF16), shape(states, F32), shape(carry, F32), shape((heads, 8, 128), F32),
                shape((heads, BLOCK, 128), F32))
        held = pl.pallas_call(
            functools.partial(kernel, n, m, groups, heads, pieces),
            out_shape=kept,
            in_specs=[hbm] * 6,
            out_specs=(vmem,) * 10,
            scratch_shapes=[
                pltpu.SMEM((heads,), F32), pltpu.VMEM(row, BF16), pltpu.VMEM(row, BF16), pltpu.VMEM((1, width), F32),
                dma((6,)),
                pltpu.VMEM((heads, BLOCK, BLOCK), F32),
                pltpu.VMEM((blocks, heads, BLOCK, BLOCK), BF16),
                pltpu.VMEM(row, F32),
                pltpu.VMEM(row, BF16),
                pltpu.VMEM(row, F32),
                pltpu.VMEM((blocks, heads, 128, 2 * BLOCK), BF16),
                pltpu.VMEM((heads, BLOCK, 128), F32),
                pltpu.VMEM(carry, F32),
                pltpu.VMEM((8, tokens), F32),
                pltpu.VMEM((max(m - 1, 1), 8, tokens), F32),
                dma((max(m - 1, 1),)), dma((max(m - 1, 1),)),
                pltpu.VMEM(states, F32), pltpu.VMEM(states, F32), pltpu.VMEM(states, F32),
            ] + scan_scratch(size, groups, hp, pieces) * 2,
            compiler_params=pltpu.CompilerParams(
                collective_id=0, has_side_effects=True, vmem_limit_bytes=32 * 2**20),
        )(*[pltpu.with_memory_space_constraint(x, pltpu.HBM) for x in (
            decay_rates, queries, key_rows, value_rows, norm_gain.reshape(1, width), out_grad)])
        return pl.pallas_call(
            functools.partial(last_kernel, heads),
            out_shape=(shape(row, BF16),) * 4,
            in_specs=[vmem] * 10,
            out_specs=(hbm,) * 4,
            scratch_shapes=[pltpu.VMEM(row, BF16), pltpu.VMEM(row, BF16), dma((2,)), dma((2, heads))],
            compiler_params=pltpu.CompilerParams(vmem_limit_bytes=16 * 2**20),
        )(*held)

    rows = P("ctx", "head")
    return jax.shard_map(
        on_device, mesh=mesh, in_specs=(rows, rows, rows, P("head"), P("head"), rows),
        out_specs=(rows,) * 4, check_vma=False)
```
